256 devices in a mesh: fsdp: 16 (over y, x), tensor: 16 (over z, core).
Axes of the slice: x: 4, y: 4, z: 8, core: 2. Of those that a mesh axis runs over, the one named last changes fastest.
Arguments:
- inputs: bfloat16 [3072, 8192], P('fsdp'), may hold values from -6 to 6
- cotangent: bfloat16 [3072, 8192], P('fsdp'), may hold values from -1.1953125 to 1.1953125
- up_tiles: bfloat16 [16, 64, 128, 128], P('tensor', 'fsdp'), may hold values from -0.25 to 0.25
- up_rows: int32 [16, 64], P('tensor', 'fsdp'), may hold values from 0 to 63, as said below
- up_cols: int32 [16, 64], P('tensor', 'fsdp'), may hold values from 0 to 15, as said below
- down_tiles: bfloat16 [16, 64, 128, 128], P('tensor', 'fsdp'), may hold values from -0.25 to 0.25
- down_rows: int32 [16, 64], P('tensor', 'fsdp'), may hold values from 0 to 15, as said below
- down_cols: int32 [16, 64], P('tensor', 'fsdp'), may hold values from 0 to 63, as said below
Outputs:
- input_grad: bfloat16 [3072, 8192], P('fsdp', 'tensor')
- up_grad: bfloat16 [16, 64, 128, 128], P('tensor', 'fsdp')
- down_grad: bfloat16 [16, 64, 128, 128], P('tensor', 'fsdp')
The draws below stay inside these ranges and needn't reach their ends.
Inputs may be any that keep to these rules, and one draw needn't show every extreme that they name: `up_rows`: together with up_cols, the positions of a group's 64 tiles are distinct; slot s is held by fsdp index s // 4. `up_cols`: see up_rows. `down_rows`: together with down_cols, the positions of a group's 64 tiles are distinct; slot s is held by fsdp index s // 4. `down_cols`: see down_rows.
All inputs are finite; a program needn't handle non-finite values.
Results may differ from the reference program's by a relative error of at most 0.015.
Values may be sent and summed in bfloat16 or wider, within the bound.
A program may use at most 128 MiB of HBM per device.

```python
import jax
import jax.numpy as jnp
from jax import lax

D = 8192
TILE = 128
TOK_DEV = 192
TOKENS = 3072
GROUPS = 16
SLOTS = 64
ROW_BLOCKS = 64
GROUP_COLS = 16
N_FSDP = 16


def tile_positions(key, row_count, col_count):
    total = row_count * col_count

    def one_group(group_key):
        first_key, second_key = jax.random.split(group_key)
        middle = (jax.random.permutation(first_key, total - 2) + 1).astype(jnp.int32)
        ends = jnp.array([0, total - 1], jnp.int32)
        picked = jnp.concatenate([ends, middle[:SLOTS - 2]])
        order = jax.random.permutation(second_key, SLOTS)
        return picked[order]
    keys = jax.random.split(key, GROUPS)
    return jax.vmap(one_group)(keys)


def draw_up_rows(key, part):
    places = tile_positions(jax.random.fold_in(key, 11), ROW_BLOCKS, GROUP_COLS)
    return (places // GROUP_COLS).astype(jnp.int32)


def draw_up_cols(key, part):
    places = tile_positions(jax.random.fold_in(key, 11), ROW_BLOCKS, GROUP_COLS)
    return (places % GROUP_COLS).astype(jnp.int32)


def draw_down_rows(key, part):
    places = tile_positions(jax.random.fold_in(key, 23), GROUP_COLS, ROW_BLOCKS)
    return (places // ROW_BLOCKS).astype(jnp.int32)


def draw_down_cols(key, part):
    places = tile_positions(jax.random.fold_in(key, 23), GROUP_COLS, ROW_BLOCKS)
    return (places % ROW_BLOCKS).astype(jnp.int32)


def block_levels(rng, extent, cuts, low, high):
    loudness, own = 1.0, jax.random.fold_in(rng, 6)
    for axis_at, shards_of in cuts:
        draws = jnp.exp(jax.random.uniform(jax.random.fold_in(own, axis_at), (shards_of,), jnp.float32, low / len(cuts), high / len(cuts)))
        loudness = loudness * jnp.repeat(draws, extent[axis_at] // shards_of).reshape([-1 if axis == axis_at else 1 for axis in range(len(extent))])
    return loudness


def scatter_about(own_key, extent, scale, reach, shards=(), kind=jnp.bfloat16):
    factor_of = block_levels(own_key, extent, shards, -0.22, 0.18) if shards else 1.0
    entries = jax.random.normal(own_key, extent, jnp.float32) * scale * factor_of
    return jnp.minimum(jnp.maximum(entries, -reach), reach).astype(kind)


def setup_inputs(seed: int = 0) -> dict:
    arg_keys = jax.random.split(jax.random.key(seed), 9)
    inputs = scatter_about(arg_keys[0], (TOKENS, D), 1.0, 6.0, ((0, 16),))
    cotangent = scatter_about(arg_keys[1], (TOKENS, D), 0.2, 1.1953125, ((0, 16),))
    up_tiles = scatter_about(arg_keys[2], (GROUPS, SLOTS, TILE, TILE), (TILE * SLOTS // GROUP_COLS) ** -0.5, 0.25, ((0, 16), (1, 16)))
    up_rows = draw_up_rows(jax.random.fold_in(arg_keys[8], 71), 0)
    up_cols = draw_up_cols(jax.random.fold_in(arg_keys[8], 71), 0)
    down_tiles = scatter_about(arg_keys[5], (GROUPS, SLOTS, TILE, TILE), (TILE * SLOTS // GROUP_COLS) ** -0.5, 0.25, ((0, 16), (1, 16)))
    down_rows = draw_down_rows(jax.random.fold_in(arg_keys[8], 71), 0)
    down_cols = draw_down_cols(jax.random.fold_in(arg_keys[8], 71), 0)
    return dict(inputs=inputs, cotangent=cotangent, up_tiles=up_tiles, up_rows=up_rows, up_cols=up_cols, down_tiles=down_tiles, down_rows=down_rows, down_cols=down_cols)


def gelu_parts(pre):
    coef = 0.7978845608028654
    inner = coef * (pre + 0.044715 * pre * pre * pre)
    tanh_val = jnp.tanh(inner)
    act = 0.5 * pre * (1.0 + tanh_val)
    slope = 0.5 * (1.0 + tanh_val) + 0.5 * pre * (1.0 - tanh_val * tanh_val) * coef * (1.0 + 3.0 * 0.044715 * pre * pre)
    return act, slope


def reference(inputs, cotangent, up_tiles, up_rows, up_cols, down_tiles, down_rows, down_cols):
    tok_count = inputs.shape[0]
    input_blocks = inputs.reshape(tok_count, ROW_BLOCKS, TILE)
    cotan_blocks = cotangent.reshape(tok_count, ROW_BLOCKS, TILE)

    def group_step(carry, group):
        w_up, r_up, c_up, w_down, r_down, c_down = group
        x_sel = jnp.take(input_blocks, r_up, axis=1).astype(jnp.float32)
        prod = jnp.einsum("tsk,skf->stf", x_sel, w_up.astype(jnp.float32))
        pre = jax.ops.segment_sum(prod, c_up, num_segments=GROUP_COLS)
        act, slope = gelu_parts(pre)
        hidden = act.astype(jnp.bfloat16)
        dy_sel = jnp.take(cotan_blocks, c_down, axis=1).astype(jnp.float32)
        back = jnp.einsum("tsk,sfk->stf", dy_sel, w_down.astype(jnp.float32))
        dhid = jax.ops.segment_sum(back, r_down, num_segments=GROUP_COLS)
        dpre = (dhid * slope).astype(jnp.bfloat16)
        h_sel = jnp.take(hidden, r_down, axis=0).astype(jnp.float32)
        h_split = h_sel.reshape(SLOTS, N_FSDP, TOK_DEV, TILE)
        dy_split = dy_sel.reshape(N_FSDP, TOK_DEV, SLOTS, TILE)
        down_part = jnp.einsum("sbtf,btsk->bsfk", h_split, dy_split).astype(jnp.bfloat16)
        down_grad = jnp.sum(down_part.astype(jnp.float32), axis=0).astype(jnp.bfloat16)
        dp_sel = jnp.take(dpre, c_up, axis=0).astype(jnp.float32)
        dp_split = dp_sel.reshape(SLOTS, N_FSDP, TOK_DEV, TILE)
        x_split = x_sel.reshape(N_FSDP, TOK_DEV, SLOTS, TILE)
        up_part = jnp.einsum("btsk,sbtf->bskf", x_split, dp_split).astype(jnp.bfloat16)
        up_grad = jnp.sum(up_part.astype(jnp.float32), axis=0).astype(jnp.bfloat16)
        back_in = jnp.einsum("stf,skf->stk", dp_sel, w_up.astype(jnp.float32))
        in_part = jax.ops.segment_sum(back_in, r_up, num_segments=ROW_BLOCKS).astype(jnp.bfloat16)
        return carry + in_part.astype(jnp.float32), (up_grad, down_grad)

    start = jnp.zeros((ROW_BLOCKS, tok_count, TILE), jnp.float32)
    total, grads = lax.scan(group_step, start, (up_tiles, up_rows, up_cols, down_tiles, down_rows, down_cols))
    input_grad = jnp.transpose(total, (1, 0, 2)).reshape(tok_count, D).astype(jnp.bfloat16)
    return input_grad, grads[0], grads[1]
```

```python
import jax
import jax.numpy as jnp
from jax import lax
from jax.experimental import pallas as pl
from jax.experimental.pallas import tpu as pltpu
from jax.sharding import PartitionSpec as P

TILE = 128
SLOTS = 64
MESH = pl.DeviceIdType.MESH
F32 = jnp.float32
BF16 = jnp.bfloat16

ORDER = (
    [(0, 0), (0, 3), (0, 1), (0, 2)]
    + [(a, b) for b in (0, 3, 1, 2) for a in (3, 1)]
    + [(2, b) for b in (0, 3, 1, 2)]
)
POS = {ab: n for n, ab in enumerate(ORDER)}
UP_ROW, UP_COL, DN_ROW, DN_COL, PREV_UP, PREV_DN, PREV_ROW, LAST_UP, LAST_DN, LAST_ROW = range(10)


def gelu_parts(pre):
    coef = 0.7978845608028654
    inner = coef * (pre + 0.044715 * pre * pre * pre)
    tanh_val = jnp.tanh(inner)
    act = 0.5 * pre * (1.0 + tanh_val)
    slope = 0.5 * (1.0 + tanh_val) + 0.5 * pre * (1.0 - tanh_val * tanh_val) * coef * (
        1.0 + 3.0 * 0.044715 * pre * pre
    )
    return act, slope


def dot_nn(a, b):
    return lax.dot_general(a, b, (((1,), (0,)), ((), ())), preferred_element_type=F32)


def dot_nt(a, b):
    return lax.dot_general(a, b, (((1,), (1,)), ((), ())), preferred_element_type=F32)


def kernel(
    x_hbm, dy_hbm, up_hbm, down_hbm, ur, uc, dr, dc,
    gin_ref, gup_ref, gdn_ref,
    x_v, dy_v, ga, gb, idx_v, tbl_v, tbl,
    pu, pd, slope_v, dp_v, dpt_v, ht_v,
    pa, pb, ra1, ra2, ra3, ra4, rb1, rb2, rb3, rb4,
    xs, rx, zc, rz,
    send_sem, recv_sem, loc_sem,
):
    f = lax.axis_index("fsdp")
    t = lax.axis_index("tensor")
    y, x = f // 4, f % 4
    z, core = t // 2, t % 2
    xp = {"fsdp": y * 4 + (x + 1) % 4}
    xm = {"fsdp": y * 4 + (x + 3) % 4}
    yp = {"fsdp": ((y + 1) % 4) * 4 + x}
    ym = {"fsdp": ((y + 3) % 4) * 4 + x}
    zp = {"tensor": ((z + 1) % 8) * 2 + core}
    zm = {"tensor": ((z + 7) % 8) * 2 + core}
    mate = {"tensor": z * 2 + 1 - core}

    count = [0]
    sent = []

    def message(src, dst, dev):
        n = count[0]
        count[0] += 1
        copy = pltpu.make_async_remote_copy(
            src_ref=src, dst_ref=dst, send_sem=send_sem.at[n], recv_sem=recv_sem.at[n],
            device_id=dev, device_id_type=MESH,
        )
        sent.append(copy)
        return copy

    own_a = pltpu.make_async_copy(up_hbm.at[0], ga.at[0], loc_sem.at[0])
    own_b = pltpu.make_async_copy(down_hbm.at[0], gb.at[0], loc_sem.at[1])
    get_x = pltpu.make_async_copy(x_v, x_v, loc_sem.at[2])
    get_dy = pltpu.make_async_copy(dy_v, dy_v, loc_sem.at[3])

    def fetch(c, _):
        src = pl.ds(pl.multiple_of(c * TILE, TILE), TILE)
        pltpu.make_async_copy(x_hbm.at[:, src], x_v.at[c], loc_sem.at[2]).start()
        pltpu.make_async_copy(dy_hbm.at[:, src], dy_v.at[c], loc_sem.at[3]).start()
        return 0

    own_a.start()
    own_b.start()

    barrier = pltpu.get_barrier_semaphore()
    for dev in (xp, xm, yp, ym, zp, zm, mate):
        pl.semaphore_signal(barrier, inc=1, device_id=dev, device_id_type=MESH)

    lane = lax.broadcasted_iota(jnp.int32, (8, TILE), 1)
    row = lax.broadcasted_iota(jnp.int32, (8, TILE), 0)
    own = jnp.zeros((8, TILE), jnp.int32)
    for r, ref in enumerate((ur, uc, dr, dc)):
        for i in range(4):
            own = jnp.where((row == r) & (lane == i), ref[0, i], own)
    idx_v[0, 0] = own
    own_a.wait()
    own_b.wait()
    pl.semaphore_wait(barrier, 7)

    class Gather:
        def __init__(self, g, first, second):
            (bp, bm), (ap, am) = first, second
            at = lambda a, b: g.at[POS[a, b]]
            half = lambda a, b, h: g.at[POS[a, b], pl.ds(2 * h, 2)]
            self.f1 = {3: message(at(0, 0), at(0, 3), bp), 1: message(at(0, 0), at(0, 1), bm)}
            self.f2 = {
                3: message(half(0, 3, 0), half(0, 2, 0), bp),
                1: message(half(0, 1, 1), half(0, 2, 1), bm),
            }
            self.s1 = {}
            self.s2 = {}
            for b in (0, 3, 1, 2):
                self.s1[3, b] = message(at(0, b), at(3, b), ap)
                self.s1[1, b] = message(at(0, b), at(1, b), am)
                self.s2[3, b] = message(half(3, b, 0), half(2, b, 0), ap)
                self.s2[1, b] = message(half(1, b, 1), half(2, b, 1), am)

    A = Gather(ga, (xp, xm), (yp, ym))
    B = Gather(gb, (yp, ym), (xp, xm))
    ix = {
        3: message(idx_v.at[0, 0], idx_v.at[0, 3], xp),
        1: message(idx_v.at[0, 0], idx_v.at[0, 1], xm),
        2: message(idx_v.at[0, 3], idx_v.at[0, 2], xp),
    }
    iy = {
        3: message(idx_v.at[0], idx_v.at[3], yp),
        1: message(idx_v.at[0], idx_v.at[1], ym),
        2: message(idx_v.at[3], idx_v.at[2], yp),
    }

    ix[3].start()
    ix[1].start()
    for b in (3, 1):
        A.f1[b].start()
        B.f1[b].start()
    for a in (3, 1):
        A.s1[a, 0].start()
        B.s1[a, 0].start()
    lax.fori_loop(0, 64, fetch, 0)
    ix[3].wait_recv()
    ix[2].start()
    zero = jnp.zeros((192, TILE), F32)
    pu[SLOTS] = zero
    pd[SLOTS] = zero
    ix[1].wait_recv()
    ix[2].wait_recv()
    iy[3].start()
    iy[1].start()

    for b in (3, 1):
        for G in (A, B):
            G.f1[b].wait_recv()
            G.f2[b].start()
            for a in (3, 1):
                G.s1[a, b].start()

    iy[3].wait_recv()
    iy[2].start()
    for G in (A, B):
        for b in (3, 1):
            G.f2[b].wait_recv()
        for a in (3, 1):
            G.s1[a, 2].start()
    iy[1].wait_recv()
    iy[2].wait_recv()

    both = jnp.zeros((8, TILE), jnp.int32)
    for v in range(4):
        for h in range(4):
            tile = idx_v[v, h]
            na, nb = POS[v, h], POS[h, v]
            moved_a = pltpu.roll(tile, 4 * na, 1) if na else tile
            moved_b = pltpu.roll(tile, 4 * nb, 1) if nb else tile
            both = both + jnp.where(row < 2, moved_a, jnp.where(row < 4, moved_b, 0))
    tbl_v[0:8] = both
    si = lax.broadcasted_iota(jnp.int32, (TILE, TILE), 0)
    li = lax.broadcasted_iota(jnp.int32, (TILE, TILE), 1)
    across = lambda r: jnp.broadcast_to(both[r : r + 1], (TILE, TILE))

    def chain(r):
        here = across(r)
        there = here.T
        prev = jnp.max(jnp.where((there == here) & (si < li), si, -1), axis=0, keepdims=True)
        last = jnp.max(jnp.where((there == li) & (si < SLOTS), si, -1), axis=0, keepdims=True)
        fix = lambda v: jnp.where(v < 0, SLOTS, v)
        return fix(prev), fix(last)

    prev_up, last_up = chain(UP_COL)
    prev_dn, last_dn = chain(DN_ROW)
    prev_row, last_row = chain(UP_ROW)
    tbl_v[PREV_UP : PREV_UP + 1] = prev_up
    tbl_v[PREV_DN : PREV_DN + 1] = prev_dn
    tbl_v[PREV_ROW : PREV_ROW + 1] = prev_row
    tbl_v[LAST_UP : LAST_UP + 1] = last_up
    tbl_v[LAST_DN : LAST_DN + 1] = last_dn
    tbl_v[LAST_ROW : LAST_ROW + 1] = last_row
    put = pltpu.make_async_copy(tbl_v, tbl, loc_sem.at[4])
    put.start()
    get_x.wait()
    get_dy.wait()
    put.wait()

    cols = lambda ref, n: ref[n]

    def take_up(n):
        d = []
        for i in range(4):
            s = n * 4 + i
            d.append(dot_nn(cols(x_v, tbl[UP_ROW, s]), ga[n, i]))
        for i in range(4):
            s = n * 4 + i
            pu[s] = d[i] + pu[tbl[PREV_UP, s]]

    def take_down(n):
        d = []
        for i in range(4):
            s = n * 4 + i
            d.append(dot_nt(cols(dy_v, tbl[DN_COL, s]), gb[n, i]))
        for i in range(4):
            s = n * 4 + i
            pd[s] = d[i] + pd[tbl[PREV_DN, s]]

    def take(n, _):
        take_up(n)
        take_down(n)
        return 0

    for k, b in enumerate((0, 3, 1, 2)):
        for G in (A, B):
            for a in (3, 1):
                G.s1[a, b].wait_recv()
                G.s2[a, b].start()
        take(k, 0)
    for k, b in enumerate((0, 3, 1, 2)):
        lax.fori_loop(4 + 2 * k, 6 + 2 * k, take, 0)
    for k, b in enumerate((0, 3, 1, 2)):
        for G in (A, B):
            for a in (3, 1):
                G.s2[a, b].wait_recv()
        take(12 + k, 0)

    def activate(c, _):
        act, slope = gelu_parts(pu[tbl[LAST_UP, c]])
        dpre = pd[tbl[LAST_DN, c]] * slope
        ht_v[c] = act.T.astype(BF16)
        dp_v[c] = dpre.astype(BF16)
        dpt_v[c] = dpre.T.astype(BF16)
        return 0

    lax.fori_loop(0, 16, activate, 0)

    def take_in(n, _):
        d = []
        for i in range(4):
            s = n * 4 + i
            d.append(dot_nt(dp_v[tbl[UP_COL, s]], ga[n, i]))
        for i in range(4):
            s = n * 4 + i
            pu[s] = d[i] + pu[tbl[PREV_ROW, s]]
        return 0

    lax.fori_loop(0, 16, take_in, 0)

    def part(dz, c, j):
        return pu[tbl[LAST_ROW, (((z + dz) % 8) * 2 + c) * 4 + j]]

    ZORDER = (4, 3, 5, 2, 6, 1, 7, 0)
    ex = {dz: message(xs.at[dz], rx.at[dz], mate) for dz in ZORDER}
    for dz in ZORDER:
        for j in range(4):
            xs[dz, j] = part(dz, 1 - core, j).astype(BF16)
        ex[dz].start()

    up_z = {}
    dn_z = {}
    for n in (4, 3, 2, 1):
        for h in range(2):
            hs = pl.ds(2 * h, 2)
            if n < 4 or h == 0:
                up_z[n, h] = message(zc.at[n, hs], rz.at[0, n - 1, hs], zp)
            if n < 4 or h == 1:
                dn_z[n, h] = message(zc.at[8 - n, hs], rz.at[1, n - 1, hs], zm)

    def ring(n):
        if n == 4:
            ex[4].wait_recv()
            for j in range(4):
                zc[4, j] = (part(4, core, j) + rx[4, j].astype(F32)).astype(BF16)
            up_z[4, 0].start()
            dn_z[4, 1].start()
            return
        ex[n].wait_recv()
        ex[8 - n].wait_recv()
        for k in range(2):
            for side, first in ((0, 1), (1, 0)):
                h = first if k == 0 else 1 - first
                came = (up_z, dn_z)[side]
                slot = n if side == 0 else 8 - n
                added = (n + 1, h) in came
                if added:
                    came[n + 1, h].wait_recv()
                for j in (2 * h, 2 * h + 1):
                    v = part(slot, core, j) + rx[slot, j].astype(F32)
                    if added:
                        v = v + rz[side, n, j].astype(F32)
                    zc[slot, j] = v.astype(BF16)
                came[n, h].start()

    def ring_end():
        ex[0].wait_recv()
        for h in range(2):
            up_z[1, h].wait_recv()
            dn_z[1, h].wait_recv()
            for j in (2 * h, 2 * h + 1):
                v = part(0, core, j) + rx[0, j].astype(F32)
                v = v + rz[0, 0, j].astype(F32) + rz[1, 0, j].astype(F32)
                gin_ref[:, j * TILE : (j + 1) * TILE] = v.astype(BF16)

    def grad_up(n):
        for i in range(4):
            s = n * 4 + i
            pa[n, i] = dot_nn(dpt_v[tbl[UP_COL, s]], cols(x_v, tbl[UP_ROW, s])).astype(BF16)

    def grad_down(n):
        for i in range(4):
            s = n * 4 + i
            pb[n, i] = dot_nn(ht_v[tbl[DN_ROW, s]], cols(dy_v, tbl[DN_COL, s])).astype(BF16)

    def add_half(p, n, h, r):
        for i in range(2):
            p[n, 2 * h + i] = (p[n, 2 * h + i].astype(F32) + r[i].astype(F32)).astype(BF16)

    class Scatter:
        def __init__(self, p, r1, r2, r3, r4, grad, first, second):
            (self.ap, self.am), (self.bp, self.bm) = first, second
            self.p, self.r1, self.r2, self.r3, self.r4, self.grad = p, r1, r2, r3, r4, grad
            at = lambda a, b: p.at[POS[a, b]]
            half = lambda a, b, h: p.at[POS[a, b], pl.ds(2 * h, 2)]
            self.m1 = {}
            self.m2 = {}
            for b in range(4):
                self.m1[1, b] = message(half(2, b, 0), r1.at[0, b], self.ap)
                self.m1[3, b] = message(half(2, b, 1), r1.at[1, b], self.am)
                self.m2[1, b] = message(at(1, b), r2.at[0, b], self.ap)
                self.m2[3, b] = message(at(3, b), r2.at[1, b], self.am)
            self.m3 = {
                1: message(half(0, 2, 0), r3.at[0], self.bp),
                3: message(half(0, 2, 1), r3.at[1], self.bm),
            }
            self.m4 = {
                1: message(at(0, 1), r4.at[0], self.bp),
                3: message(at(0, 3), r4.at[1], self.bm),
            }

        def far(self, b):
            self.grad(POS[2, b])
            self.m1[1, b].start()
            self.m1[3, b].start()

        def near(self, a, b):
            self.grad(POS[a, b])
            self.m1[a, b].wait_recv()
            h = 0 if a == 1 else 1
            add_half(self.p, POS[a, b], h, self.r1.at[h, b])
            self.m2[a, b].start()

        def total(self, b):
            self.m2[1, b].wait_recv()
            self.m2[3, b].wait_recv()
            n = POS[0, b]
            for i in range(4):
                v = self.p[n, i].astype(F32) + self.r2[0, b, i].astype(F32)
                v = v + self.r2[1, b, i].astype(F32)
                self.p[n, i] = v.astype(BF16)
            if b == 2:
                self.m3[1].start()
                self.m3[3].start()

        def turn(self, b):
            h = 0 if b == 1 else 1
            self.m3[b].wait_recv()
            add_half(self.p, POS[0, b], h, self.r3.at[h])
            self.m4[b].start()

        def end(self, out, flip):
            self.m4[1].wait_recv()
            self.m4[3].wait_recv()
            for i in range(4):
                v = self.p[POS[0, 0], i].astype(F32) + self.r4[0, i].astype(F32)
                v = v + self.r4[1, i].astype(F32)
                out[0, i] = (v.T if flip else v).astype(BF16)

    U = Scatter(pa, ra1, ra2, ra3, ra4, grad_up, (yp, ym), (xp, xm))
    D = Scatter(pb, rb1, rb2, rb3, rb4, grad_down, (xp, xm), (yp, ym))

    for b in (2, 1, 3, 0):
        U.far(b)
        D.far(b)
    ring(4)
    for b in (2, 1):
        for a in (1, 3):
            U.near(a, b)
            D.near(a, b)
    ring(3)
    for b in (3, 0):
        for a in (1, 3):
            U.near(a, b)
            D.near(a, b)
    ring(2)
    for b in (2, 1, 3, 0):
        grad_up(POS[0, b])
        grad_down(POS[0, b])
    for S in (U, D):
        S.total(2)
    ring(1)
    for b in (1, 3):
        for S in (U, D):
            S.total(b)
            S.turn(b)
    for S in (U, D):
        S.total(0)
    ring_end()
    U.end(gup_ref, True)
    D.end(gdn_ref, False)
    for copy in sent:
        copy.wait_send()
    assert count[0] <= 128


def on_device(inputs, cotangent, up_tiles, up_rows, up_cols, down_tiles, down_rows, down_cols):
    tok = inputs.shape[0]
    width = inputs.shape[1]
    hbm = pl.BlockSpec(memory_space=pl.ANY)
    vmem = pl.BlockSpec(memory_space=pltpu.VMEM)
    smem = pl.BlockSpec(memory_space=pltpu.SMEM)
    tiles = lambda *n: pltpu.VMEM((*n, TILE, TILE), BF16)
    blocks = lambda *n: pltpu.VMEM((*n, tok, TILE), BF16)
    scatter_bufs = [tiles(2, 4, 2), tiles(2, 4, 4), tiles(2, 2), tiles(2, 4)]
    return pl.pallas_call(
        kernel,
        out_shape=(
            jax.ShapeDtypeStruct((tok, 4 * TILE), BF16),
            jax.ShapeDtypeStruct((1, 4, TILE, TILE), BF16),
            jax.ShapeDtypeStruct((1, 4, TILE, TILE), BF16),
        ),
        in_specs=[hbm, hbm, hbm, hbm, smem, smem, smem, smem],
        out_specs=(vmem, vmem, vmem),
        scratch_shapes=[
            blocks(width // TILE),
            blocks(width // TILE),
            tiles(16, 4),
            tiles(16, 4),
            pltpu.VMEM((4, 4, 8, TILE), jnp.int32),
            pltpu.VMEM((16, TILE), jnp.int32),
            pltpu.SMEM((16, TILE), jnp.int32),
            pltpu.VMEM((SLOTS + 1, tok, TILE), F32),
            pltpu.VMEM((SLOTS + 1, tok, TILE), F32),
            pltpu.VMEM((8, TILE), F32),
            blocks(16),
            pltpu.VMEM((16, TILE, tok), BF16),
            pltpu.VMEM((16, TILE, tok), BF16),
            tiles(16, 4),
            tiles(16, 4),
            *scatter_bufs,
            *scatter_bufs,
            blocks(8, 4),
            blocks(8, 4),
            blocks(8, 4),
            blocks(2, 4, 4),
            pltpu.SemaphoreType.DMA((128,)),
            pltpu.SemaphoreType.DMA((128,)),
            pltpu.SemaphoreType.DMA((8,)),
        ],
        compiler_params=pltpu.CompilerParams(
            collective_id=0, has_side_effects=True, vmem_limit_bytes=60 * 1024 * 1024
        ),
    )(inputs, cotangent, up_tiles, down_tiles, up_rows, up_cols, down_rows, down_cols)


def solution(mesh):
    placed = (
        P("fsdp", None),
        P("fsdp", None),
        P("tensor", "fsdp", None, None),
        P("tensor", "fsdp"),
        P("tensor", "fsdp"),
        P("tensor", "fsdp", None, None),
        P("tensor", "fsdp"),
        P("tensor", "fsdp"),
    )
    return jax.shard_map(
        on_device,
        mesh=mesh,
        in_specs=placed,
        out_specs=(
            P("fsdp", "tensor"),
            P("tensor", "fsdp", None, None),
            P("tensor", "fsdp", None, None),
        ),
        check_vma=False,
    )
```

```python
import jax
import jax.numpy as jnp
from jax import lax
from jax.experimental import pallas as pl
from jax.experimental.pallas import tpu as pltpu
from jax.sharding import PartitionSpec as P

TILE = 128
SLOTS = 64
MESH = pl.DeviceIdType.MESH
F32 = jnp.float32
BF16 = jnp.bfloat16

ORDER = (
    [(0, 0), (0, 3), (0, 1), (0, 2)]
    + [(a, b) for b in (0, 3, 1, 2) for a in (3, 1)]
    + [(2, b) for b in (0, 3, 1, 2)]
)
POS = {ab: n for n, ab in enumerate(ORDER)}
UP_ROW, UP_COL, DN_ROW, DN_COL, PREV_UP, PREV_DN, PREV_ROW, LAST_UP, LAST_DN, LAST_ROW = range(10)


def gelu_parts(pre):
    coef = 0.7978845608028654
    inner = coef * (pre + 0.044715 * pre * pre * pre)
    tanh_val = jnp.tanh(inner)
    act = 0.5 * pre * (1.0 + tanh_val)
    slope = 0.5 * (1.0 + tanh_val) + 0.5 * pre * (1.0 - tanh_val * tanh_val) * coef * (
        1.0 + 3.0 * 0.044715 * pre * pre
    )
    return act, slope


def dot_nn(a, b):
    return lax.dot_general(a, b, (((1,), (0,)), ((), ())), preferred_element_type=F32)


def dot_nt(a, b):
    return lax.dot_general(a, b, (((1,), (1,)), ((), ())), preferred_element_type=F32)


def kernel(
    x_hbm, dy_hbm, up_hbm, down_hbm, ur, uc, dr, dc,
    gin_ref, gup_ref, gdn_ref,
    x_v, dy_v, ga, gb, idx_v, tbl_v, tbl,
    pu, pd, slope_v, dp_v, dpt_v, ht_v,
    pa, pb, ra1, ra2, ra3, ra4, rb1, rb2, rb3, rb4,
    xs, rx, zc, rz,
    send_sem, recv_sem, loc_sem,
):
    f = lax.axis_index("fsdp")
    t = lax.axis_index("tensor")
    y, x = f // 4, f % 4
    z, core = t // 2, t % 2
    xp = {"fsdp": y * 4 + (x + 1) % 4}
    xm = {"fsdp": y * 4 + (x + 3) % 4}
    yp = {"fsdp": ((y + 1) % 4) * 4 + x}
    ym = {"fsdp": ((y + 3) % 4) * 4 + x}
    zp = {"tensor": ((z + 1) % 8) * 2 + core}
    zm = {"tensor": ((z + 7) % 8) * 2 + core}
    mate = {"tensor": z * 2 + 1 - core}

    count = [0]
    sent = []

    def message(src, dst, dev):
        n = count[0]
        count[0] += 1
        copy = pltpu.make_async_remote_copy(
            src_ref=src, dst_ref=dst, send_sem=send_sem.at[n], recv_sem=recv_sem.at[n],
            device_id=dev, device_id_type=MESH,
        )
        sent.append(copy)
        return copy

    own_a = pltpu.make_async_copy(up_hbm.at[0], ga.at[0], loc_sem.at[0])
    own_b = pltpu.make_async_copy(down_hbm.at[0], gb.at[0], loc_sem.at[1])
    get_x = pltpu.make_async_copy(x_v, x_v, loc_sem.at[2])
    get_dy = pltpu.make_async_copy(dy_v, dy_v, loc_sem.at[3])

    def fetch(c, _):
        src = pl.ds(pl.multiple_of(c * TILE, TILE), TILE)
        pltpu.make_async_copy(x_hbm.at[:, src], x_v.at[c], loc_sem.at[2]).start()
        pltpu.make_async_copy(dy_hbm.at[:, src], dy_v.at[c], loc_sem.at[3]).start()
        return 0

    own_a.start()
    own_b.start()

    barrier = pltpu.get_barrier_semaphore()
    for dev in (xp, xm, yp, ym, zp, zm, mate):
        pl.semaphore_signal(barrier, inc=1, device_id=dev, device_id_type=MESH)

    lane = lax.broadcasted_iota(jnp.int32, (8, TILE), 1)
    row = lax.broadcasted_iota(jnp.int32, (8, TILE), 0)
    own = jnp.zeros((8, TILE), jnp.int32)
    for r, ref in enumerate((ur, uc, dr, dc)):
        for i in range(4):
            own = jnp.where((row == r) & (lane == i), ref[0, i], own)
    idx_v[0, 0] = own
    own_a.wait()
    own_b.wait()
    pl.semaphore_wait(barrier, 7)

    class Gather:
        def __init__(self, g):
            self.own_first, self.own_second = [], []
            self.f1, self.f2, self.s1, self.s2 = {}, {}, {}, {}
            for o, bp, bm, ap, am in ((0, xp, xm, yp, ym), (2, yp, ym, xp, xm)):
                at = lambda a, b: g.at[POS[a, b], pl.ds(o, 2)]
                half = lambda a, b, h: g.at[POS[a, b], pl.ds(o + h, 1)]
                self.f1[o, 3] = message(at(0, 0), at(0, 3), bp)
                self.f1[o, 1] = message(at(0, 0), at(0, 1), bm)
                self.f2[o, 3] = message(half(0, 3, 0), half(0, 2, 0), bp)
                self.f2[o, 1] = message(half(0, 1, 1), half(0, 2, 1), bm)
                for b in (0, 3, 1, 2):
                    self.s1[o, 3, b] = message(at(0, b), at(3, b), ap)
                    self.s1[o, 1, b] = message(at(0, b), at(1, b), am)
                    self.s2[o, 3, b] = message(half(3, b, 0), half(2, b, 0), ap)
                    self.s2[o, 1, b] = message(half(1, b, 1), half(2, b, 1), am)

        def send_first(self):
            for b in (3, 1):
                for o in (0, 2):
                    self.f1[o, b].start()

        def send_second(self, b):
            for a in (3, 1):
                for o in (0, 2):
                    self.s1[o, a, b].start()

        def turn(self):
            for b in (3, 1):
                for o in (0, 2):
                    self.f1[o, b].wait_recv()
                    self.f2[o, b].start()
                self.send_second(b)

        def opposite(self):
            for b in (3, 1):
                for o in (0, 2):
                    self.f2[o, b].wait_recv()
            self.send_second(2)

        def forward(self, b):
            for a in (3, 1):
                for o in (0, 2):
                    self.s1[o, a, b].wait_recv()
                    self.s2[o, a, b].start()

        def close(self, b):
            for a in (3, 1):
                for o in (0, 2):
                    self.s2[o, a, b].wait_recv()

    A = Gather(ga)
    B = Gather(gb)
    ix = {
        3: message(idx_v.at[0, 0], idx_v.at[0, 3], xp),
        1: message(idx_v.at[0, 0], idx_v.at[0, 1], xm),
        2: message(idx_v.at[0, 3], idx_v.at[0, 2], xp),
    }
    iy = {
        3: message(idx_v.at[0], idx_v.at[3], yp),
        1: message(idx_v.at[0], idx_v.at[1], ym),
        2: message(idx_v.at[3], idx_v.at[2], yp),
    }

    ix[3].start()
    ix[1].start()
    A.send_first()
    A.send_second(0)
    lax.fori_loop(0, 64, fetch, 0)
    ix[3].wait_recv()
    ix[2].start()
    zero = jnp.zeros((192, TILE), F32)
    pu[SLOTS] = zero
    pd[SLOTS] = zero
    ix[1].wait_recv()
    ix[2].wait_recv()
    iy[3].start()
    iy[1].start()
    A.turn()
    iy[3].wait_recv()
    iy[2].start()
    A.opposite()
    B.send_first()
    iy[1].wait_recv()
    iy[2].wait_recv()

    both = jnp.zeros((8, TILE), jnp.int32)
    early = (lane & 3) < 2
    for v in range(4):
        for h in range(4):
            tile = idx_v[v, h]
            na, nb = POS[v, h], POS[h, v]
            moved_a = pltpu.roll(tile, 4 * na, 1) if na else tile
            moved_b = pltpu.roll(tile, 4 * nb, 1) if nb else tile
            both = both + jnp.where(early, moved_a, moved_b)
    tbl_v[0:8] = both
    si = lax.broadcasted_iota(jnp.int32, (TILE, TILE), 0)
    li = lax.broadcasted_iota(jnp.int32, (TILE, TILE), 1)
    across = lambda r: jnp.broadcast_to(both[r : r + 1], (TILE, TILE))

    def chain(r):
        here = across(r)
        there = here.T
        prev = jnp.max(jnp.where((there == here) & (si < li), si, -1), axis=0, keepdims=True)
        last = jnp.max(jnp.where((there == li) & (si < SLOTS), si, -1), axis=0, keepdims=True)
        fix = lambda v: jnp.where(v < 0, SLOTS, v)
        return fix(prev), fix(last)

    prev_up, last_up = chain(UP_COL)
    prev_dn, last_dn = chain(DN_ROW)
    prev_row, last_row = chain(UP_ROW)
    tbl_v[PREV_UP : PREV_UP + 1] = prev_up
    tbl_v[PREV_DN : PREV_DN + 1] = prev_dn
    tbl_v[PREV_ROW : PREV_ROW + 1] = prev_row
    tbl_v[LAST_UP : LAST_UP + 1] = last_up
    tbl_v[LAST_DN : LAST_DN + 1] = last_dn
    tbl_v[LAST_ROW : LAST_ROW + 1] = last_row
    put = pltpu.make_async_copy(tbl_v, tbl, loc_sem.at[4])
    put.start()
    get_x.wait()
    get_dy.wait()
    put.wait()

    cols = lambda ref, n: ref[n]

    def take_up(n):
        d = []
        for i in range(4):
            s = n * 4 + i
            d.append(dot_nn(cols(x_v, tbl[UP_ROW, s]), ga[n, i]))
        for i in range(4):
            s = n * 4 + i
            pu[s] = d[i] + pu[tbl[PREV_UP, s]]

    def take_down(n):
        d = []
        for i in range(4):
            s = n * 4 + i
            d.append(dot_nt(cols(dy_v, tbl[DN_COL, s]), gb[n, i]))
        for i in range(4):
            s = n * 4 + i
            pd[s] = d[i] + pd[tbl[PREV_DN, s]]

    def grad_up(n):
        for i in range(4):
            s = n * 4 + i
            pa[n, i] = dot_nn(dpt_v[tbl[UP_COL, s]], cols(x_v, tbl[UP_ROW, s])).astype(BF16)

    def grad_down(n):
        for i in range(4):
            s = n * 4 + i
            pb[n, i] = dot_nn(ht_v[tbl[DN_ROW, s]], cols(dy_v, tbl[DN_COL, s])).astype(BF16)

    def looped(first, end, step):
        def body(n, _):
            step(n)
            return 0

        lax.fori_loop(first, end, body, 0)

    def add_tile(p, n, s, r):
        p[n, s] = (p[n, s].astype(F32) + r.astype(F32)).astype(BF16)

    class Scatter:
        def __init__(self, p, r1, r2, r3, r4):
            self.p, self.r1, self.r2, self.r3, self.r4 = p, r1, r2, r3, r4
            self.m1, self.m2, self.m3, self.m4 = {}, {}, {}, {}
            for o, ap, am, bp, bm in ((0, yp, ym, xp, xm), (2, xp, xm, yp, ym)):
                at = lambda a, b: p.at[POS[a, b], pl.ds(o, 2)]
                half = lambda a, b, h: p.at[POS[a, b], pl.ds(o + h, 1)]
                k = o // 2
                for b in range(4):
                    self.m1[o, 1, b] = message(half(2, b, 0), r1.at[k, 0, b], ap)
                    self.m1[o, 3, b] = message(half(2, b, 1), r1.at[k, 1, b], am)
                    self.m2[o, 1, b] = message(at(1, b), r2.at[k, 0, b], ap)
                    self.m2[o, 3, b] = message(at(3, b), r2.at[k, 1, b], am)
                self.m3[o, 1] = message(half(0, 2, 0), r3.at[k, 0], bp)
                self.m3[o, 3] = message(half(0, 2, 1), r3.at[k, 1], bm)
                self.m4[o, 1] = message(at(0, 1), r4.at[k, 0], bp)
                self.m4[o, 3] = message(at(0, 3), r4.at[k, 1], bm)

        def far(self, b):
            for a in (1, 3):
                for o in (0, 2):
                    self.m1[o, a, b].start()

        def near(self, a, b):
            h = 0 if a == 1 else 1
            for o in (0, 2):
                self.m1[o, a, b].wait_recv()
                add_tile(self.p, POS[a, b], o + h, self.r1[o // 2, h, b, 0])
                self.m2[o, a, b].start()

        def total(self, b):
            n = POS[0, b]
            for o in (0, 2):
                self.m2[o, 1, b].wait_recv()
                self.m2[o, 3, b].wait_recv()
                for i in range(2):
                    v = self.p[n, o + i].astype(F32) + self.r2[o // 2, 0, b, i].astype(F32)
                    v = v + self.r2[o // 2, 1, b, i].astype(F32)
                    self.p[n, o + i] = v.astype(BF16)
                if b == 2:
                    self.m3[o, 1].start()
                    self.m3[o, 3].start()

        def turn(self, b):
            h = 0 if b == 1 else 1
            for o in (0, 2):
                self.m3[o, b].wait_recv()
                add_tile(self.p, POS[0, b], o + h, self.r3[o // 2, h, 0])
                self.m4[o, b].start()

        def end(self, out, flip):
            for o in (0, 2):
                self.m4[o, 1].wait_recv()
                self.m4[o, 3].wait_recv()
                for i in range(2):
                    v = self.p[POS[0, 0], o + i].astype(F32) + self.r4[o // 2, 0, i].astype(F32)
                    v = v + self.r4[o // 2, 1, i].astype(F32)
                    out[0, o + i] = (v.T if flip else v).astype(BF16)

    U = Scatter(pa, ra1, ra2, ra3, ra4)
    D = Scatter(pb, rb1, rb2, rb3, rb4)

    for k, b in enumerate((0, 3, 1, 2)):
        A.forward(b)
        if k == 1:
            B.send_second(0)
        take_up(k)
    B.turn()
    looped(4, 12, take_up)
    B.opposite()
    for k, b in enumerate((0, 3, 1, 2)):
        A.close(b)
        take_up(12 + k)
    B.forward(0)

    def activate(c):
        act, slope = gelu_parts(pu[tbl[LAST_UP, c]])
        slope_v[c] = slope
        ht_v[c] = act.T.astype(BF16)

    looped(0, 16, activate)

    for b in (3, 1, 2):
        B.forward(b)
    for b in (2, 1, 3, 0):
        grad_down(POS[2, b])
        D.far(b)
    looped(0, 12, take_down)
    looped(0, 12, grad_down)
    for k, b in enumerate((0, 3, 1, 2)):
        B.close(b)
        take_down(12 + k)

    def back(c):
        dpre = pd[tbl[LAST_DN, c]] * slope_v[c]
        dp_v[c] = dpre.astype(BF16)
        dpt_v[c] = dpre.T.astype(BF16)

    looped(0, 16, back)
    for b in (2, 1, 3, 0):
        grad_up(POS[2, b])
        U.far(b)

    def take_in(n, _):
        d = []
        for i in range(4):
            s = n * 4 + i
            d.append(dot_nt(dp_v[tbl[UP_COL, s]], ga[n, i]))
        for i in range(4):
            s = n * 4 + i
            pu[s] = d[i] + pu[tbl[PREV_ROW, s]]
        return 0

    lax.fori_loop(0, 16, take_in, 0)

    def part(dz, c, j):
        return pu[tbl[LAST_ROW, (((z + dz) % 8) * 2 + c) * 4 + j]]

    ZORDER = (4, 3, 5, 2, 6, 1, 7, 0)
    ex = {dz: message(xs.at[dz], rx.at[dz], mate) for dz in ZORDER}
    for dz in ZORDER:
        for j in range(4):
            xs[dz, j] = part(dz, 1 - core, j).astype(BF16)
        ex[dz].start()

    up_z = {}
    dn_z = {}
    for n in (4, 3, 2, 1):
        for h in range(2):
            hs = pl.ds(2 * h, 2)
            if n < 4 or h == 0:
                up_z[n, h] = message(zc.at[n, hs], rz.at[0, n - 1, hs], zp)
            if n < 4 or h == 1:
                dn_z[n, h] = message(zc.at[8 - n, hs], rz.at[1, n - 1, hs], zm)

    def ring(n):
        if n == 4:
            ex[4].wait_recv()
            for j in range(4):
                zc[4, j] = (part(4, core, j) + rx[4, j].astype(F32)).astype(BF16)
            up_z[4, 0].start()
            dn_z[4, 1].start()
            return
        ex[n].wait_recv()
        ex[8 - n].wait_recv()
        for k in range(2):
            for side, first in ((0, 1), (1, 0)):
                h = first if k == 0 else 1 - first
                came = (up_z, dn_z)[side]
                slot = n if side == 0 else 8 - n
                added = (n + 1, h) in came
                if added:
                    came[n + 1, h].wait_recv()
                for j in (2 * h, 2 * h + 1):
                    v = part(slot, core, j) + rx[slot, j].astype(F32)
                    if added:
                        v = v + rz[side, n, j].astype(F32)
                    zc[slot, j] = v.astype(BF16)
                came[n, h].start()

    def ring_end():
        ex[0].wait_recv()
        for h in range(2):
            up_z[1, h].wait_recv()
            dn_z[1, h].wait_recv()
            for j in (2 * h, 2 * h + 1):
                v = part(0, core, j) + rx[0, j].astype(F32)
                v = v + rz[0, 0, j].astype(F32) + rz[1, 0, j].astype(F32)
                gin_ref[:, j * TILE : (j + 1) * TILE] = v.astype(BF16)

    ring(4)
    for b in (2, 1):
        for a in (1, 3):
            grad_up(POS[a, b])
            U.near(a, b)
            D.near(a, b)
    ring(3)
    for b in (3, 0):
        for a in (1, 3):
            grad_up(POS[a, b])
            U.near(a, b)
            D.near(a, b)
    ring(2)
    for b in (2, 1, 3, 0):
        grad_up(POS[0, b])
    for S in (U, D):
        S.total(2)
    ring(1)
    for b in (1, 3):
        for S in (U, D):
            S.total(b)
            S.turn(b)
    for S in (U, D):
        S.total(0)
    ring_end()
    U.end(gup_ref, True)
    D.end(gdn_ref, False)
    for copy in sent:
        copy.wait_send()
    assert count[0] <= 192


def on_device(inputs, cotangent, up_tiles, up_rows, up_cols, down_tiles, down_rows, down_cols):
    tok = inputs.shape[0]
    width = inputs.shape[1]
    hbm = pl.BlockSpec(memory_space=pl.ANY)
    vmem = pl.BlockSpec(memory_space=pltpu.VMEM)
    smem = pl.BlockSpec(memory_space=pltpu.SMEM)
    tiles = lambda *n: pltpu.VMEM((*n, TILE, TILE), BF16)
    blocks = lambda *n: pltpu.VMEM((*n, tok, TILE), BF16)
    scatter_bufs = [tiles(2, 2, 4, 1), tiles(2, 2, 4, 2), tiles(2, 2, 1), tiles(2, 2, 2)]
    return pl.pallas_call(
        kernel,
        out_shape=(
            jax.ShapeDtypeStruct((tok, 4 * TILE), BF16),
            jax.ShapeDtypeStruct((1, 4, TILE, TILE), BF16),
            jax.ShapeDtypeStruct((1, 4, TILE, TILE), BF16),
        ),
        in_specs=[hbm, hbm, hbm, hbm, smem, smem, smem, smem],
        out_specs=(vmem, vmem, vmem),
        scratch_shapes=[
            blocks(width // TILE),
            blocks(width // TILE),
            tiles(16, 4),
            tiles(16, 4),
            pltpu.VMEM((4, 4, 8, TILE), jnp.int32),
            pltpu.VMEM((16, TILE), jnp.int32),
            pltpu.SMEM((16, TILE), jnp.int32),
            pltpu.VMEM((SLOTS + 1, tok, TILE), F32),
            pltpu.VMEM((SLOTS + 1, tok, TILE), F32),
            pltpu.VMEM((16, tok, TILE), F32),
            blocks(16),
            pltpu.VMEM((16, TILE, tok), BF16),
            pltpu.VMEM((16, TILE, tok), BF16),
            tiles(16, 4),
            tiles(16, 4),
            *scatter_bufs,
            *scatter_bufs,
            blocks(8, 4),
            blocks(8, 4),
            blocks(8, 4),
            blocks(2, 4, 4),
            pltpu.SemaphoreType.DMA((192,)),
            pltpu.SemaphoreType.DMA((192,)),
            pltpu.SemaphoreType.DMA((8,)),
        ],
        compiler_params=pltpu.CompilerParams(
            collective_id=0, has_side_effects=True, vmem_limit_bytes=60 * 1024 * 1024
        ),
    )(inputs, cotangent, up_tiles, down_tiles, up_rows, up_cols, down_rows, down_cols)


def solution(mesh):
    placed = (
        P("fsdp", None),
        P("fsdp", None),
        P("tensor", "fsdp", None, None),
        P("tensor", "fsdp"),
        P("tensor", "fsdp"),
        P("tensor", "fsdp", None, None),
        P("tensor", "fsdp"),
        P("tensor", "fsdp"),
    )
    return jax.shard_map(
        on_device,
        mesh=mesh,
        in_specs=placed,
        out_specs=(
            P("fsdp", "tensor"),
            P("tensor", "fsdp", None, None),
            P("tensor", "fsdp", None, None),
        ),
        check_vma=False,
    )
```

```python
import jax
import jax.numpy as jnp
from jax import lax
from jax.experimental import pallas as pl
from jax.experimental.pallas import tpu as pltpu
from jax.sharding import PartitionSpec as P

TILE = 128
SLOTS = 64
MESH = pl.DeviceIdType.MESH
F32 = jnp.float32
BF16 = jnp.bfloat16

ORDER = (
    [(0, 0), (0, 3), (0, 1), (0, 2)]
    + [(a, b) for b in (0, 3, 1, 2) for a in (3, 1)]
    + [(2, b) for b in (0, 3, 1, 2)]
)
POS = {ab: n for n, ab in enumerate(ORDER)}
UP_ROW, UP_COL, DN_ROW, DN_COL, PREV_UP, PREV_DN, PREV_ROW, LAST_UP, LAST_DN, LAST_ROW = range(10)


def gelu_parts(pre):
    coef = 0.7978845608028654
    inner = coef * (pre + 0.044715 * pre * pre * pre)
    tanh_val = jnp.tanh(inner)
    act = 0.5 * pre * (1.0 + tanh_val)
    slope = 0.5 * (1.0 + tanh_val) + 0.5 * pre * (1.0 - tanh_val * tanh_val) * coef * (
        1.0 + 3.0 * 0.044715 * pre * pre
    )
    return act, slope


def dot_nn(a, b):
    return lax.dot_general(a, b, (((1,), (0,)), ((), ())), preferred_element_type=F32)


def dot_nt(a, b):
    return lax.dot_general(a, b, (((1,), (1,)), ((), ())), preferred_element_type=F32)


def kernel(
    x_hbm, dy_hbm, up_hbm, down_hbm, ur, uc, dr, dc,
    gin_ref, gup_ref, gdn_ref,
    x_v, dy_v, ga, gb, idx_v, tbl_v, tbl,
    pu, pd, slope_v, dp_v, dpt_v, ht_v,
    pa, pb, ra1, ra2, ra3, ra4, rb1, rb2, rb3, rb4,
    xs, rx, zc, rz,
    send_sem, recv_sem, loc_sem,
):
    f = lax.axis_index("fsdp")
    t = lax.axis_index("tensor")
    y, x = f // 4, f % 4
    z, core = t // 2, t % 2
    xp = {"fsdp": y * 4 + (x + 1) % 4}
    xm = {"fsdp": y * 4 + (x + 3) % 4}
    yp = {"fsdp": ((y + 1) % 4) * 4 + x}
    ym = {"fsdp": ((y + 3) % 4) * 4 + x}
    zp = {"tensor": ((z + 1) % 8) * 2 + core}
    zm = {"tensor": ((z + 7) % 8) * 2 + core}
    mate = {"tensor": z * 2 + 1 - core}

    count = [0]
    sent = []

    def message(src, dst, dev):
        n = count[0]
        count[0] += 1
        copy = pltpu.make_async_remote_copy(
            src_ref=src, dst_ref=dst, send_sem=send_sem.at[n], recv_sem=recv_sem.at[n],
            device_id=dev, device_id_type=MESH,
        )
        sent.append(copy)
        return copy

    own_a = pltpu.make_async_copy(up_hbm.at[0], ga.at[0], loc_sem.at[0])
    own_b = pltpu.make_async_copy(down_hbm.at[0], gb.at[0], loc_sem.at[1])
    get_x = pltpu.make_async_copy(x_v, x_v, loc_sem.at[2])
    get_dy = pltpu.make_async_copy(dy_v, dy_v, loc_sem.at[3])

    def fetch(c, _):
        src = pl.ds(pl.multiple_of(c * TILE, TILE), TILE)
        pltpu.make_async_copy(x_hbm.at[:, src], x_v.at[c], loc_sem.at[2]).start()
        pltpu.make_async_copy(dy_hbm.at[:, src], dy_v.at[c], loc_sem.at[3]).start()
        return 0

    barrier = pltpu.get_barrier_semaphore()
    for dev in (xp, xm, yp, ym, zp, zm, mate):
        pl.semaphore_signal(barrier, inc=1, device_id=dev, device_id_type=MESH)
    own_a.start()
    own_b.start()

    lane = lax.broadcasted_iota(jnp.int32, (8, TILE), 1)
    row = lax.broadcasted_iota(jnp.int32, (8, TILE), 0)
    own = jnp.zeros((8, TILE), jnp.int32)
    for r, ref in enumerate((ur, uc, dr, dc)):
        for i in range(4):
            own = jnp.where((row == r) & (lane == i), ref[0, i], own)
    idx_v[0, 0] = own
    pl.semaphore_wait(barrier, 7)

    class Gather:
        def __init__(self, g, own, first, second):
            (bp, bm), (ap, am) = first, second
            at = lambda a, b: g.at[POS[a, b]]
            half = lambda a, b, h: g.at[POS[a, b], pl.ds(2 * h, 2)]
            self.f1 = {3: message(own, at(0, 3), bp), 1: message(own, at(0, 1), bm)}
            self.f2 = {
                3: message(half(0, 3, 0), half(0, 2, 0), bp),
                1: message(half(0, 1, 1), half(0, 2, 1), bm),
            }
            self.s1 = {}
            self.s2 = {}
            for b in (0, 3, 1, 2):
                src = at(0, b) if b else own
                self.s1[3, b] = message(src, at(3, b), ap)
                self.s1[1, b] = message(src, at(1, b), am)
                self.s2[3, b] = message(half(3, b, 0), half(2, b, 0), ap)
                self.s2[1, b] = message(half(1, b, 1), half(2, b, 1), am)

    A = Gather(ga, up_hbm.at[0], (xp, xm), (yp, ym))
    B = Gather(gb, down_hbm.at[0], (yp, ym), (xp, xm))
    ix = {
        3: message(idx_v.at[0, 0], idx_v.at[0, 3], xp),
        1: message(idx_v.at[0, 0], idx_v.at[0, 1], xm),
        2: message(idx_v.at[0, 3], idx_v.at[0, 2], xp),
    }
    iy = {
        3: message(idx_v.at[0], idx_v.at[3], yp),
        1: message(idx_v.at[0], idx_v.at[1], ym),
        2: message(idx_v.at[3], idx_v.at[2], yp),
    }

    ix[3].start()
    ix[1].start()
    for b in (3, 1):
        A.f1[b].start()
        B.f1[b].start()
    for a in (3, 1):
        A.s1[a, 0].start()
        B.s1[a, 0].start()
    lax.fori_loop(0, 64, fetch, 0)
    ix[3].wait_recv()
    ix[2].start()
    zero = jnp.zeros((192, TILE), F32)
    pu[SLOTS] = zero
    pd[SLOTS] = zero
    ix[1].wait_recv()
    ix[2].wait_recv()
    iy[3].start()
    iy[1].start()

    for b in (3, 1):
        for G in (A, B):
            G.f1[b].wait_recv()
            G.f2[b].start()
            for a in (3, 1):
                G.s1[a, b].start()

    iy[3].wait_recv()
    iy[2].start()
    for G in (A, B):
        for b in (3, 1):
            G.f2[b].wait_recv()
        for a in (3, 1):
            G.s1[a, 2].start()
    iy[1].wait_recv()
    iy[2].wait_recv()

    both = jnp.zeros((8, TILE), jnp.int32)
    for v in range(4):
        for h in range(4):
            tile = idx_v[v, h]
            na, nb = POS[v, h], POS[h, v]
            moved_a = pltpu.roll(tile, 4 * na, 1) if na else tile
            moved_b = pltpu.roll(tile, 4 * nb, 1) if nb else tile
            both = both + jnp.where(row < 2, moved_a, jnp.where(row < 4, moved_b, 0))
    tbl_v[0:8] = both
    si = lax.broadcasted_iota(jnp.int32, (TILE, TILE), 0)
    li = lax.broadcasted_iota(jnp.int32, (TILE, TILE), 1)
    across = lambda r: jnp.broadcast_to(both[r : r + 1], (TILE, TILE))

    def chain(r):
        here = across(r)
        there = here.T
        prev = jnp.max(jnp.where((there == here) & (si < li), si, -1), axis=0, keepdims=True)
        last = jnp.max(jnp.where((there == li) & (si < SLOTS), si, -1), axis=0, keepdims=True)
        fix = lambda v: jnp.where(v < 0, SLOTS, v)
        return fix(prev), fix(last)

    prev_up, last_up = chain(UP_COL)
    prev_dn, last_dn = chain(DN_ROW)
    prev_row, last_row = chain(UP_ROW)
    tbl_v[PREV_UP : PREV_UP + 1] = prev_up
    tbl_v[PREV_DN : PREV_DN + 1] = prev_dn
    tbl_v[PREV_ROW : PREV_ROW + 1] = prev_row
    tbl_v[LAST_UP : LAST_UP + 1] = last_up
    tbl_v[LAST_DN : LAST_DN + 1] = last_dn
    tbl_v[LAST_ROW : LAST_ROW + 1] = last_row
    put = pltpu.make_async_copy(tbl_v, tbl, loc_sem.at[4])
    put.start()
    get_x.wait()
    get_dy.wait()
    own_a.wait()
    own_b.wait()
    put.wait()

    cols = lambda ref, n: ref[n]

    def take_up(n):
        d = []
        for i in range(4):
            s = n * 4 + i
            d.append(dot_nn(cols(x_v, tbl[UP_ROW, s]), ga[n, i]))
        for i in range(4):
            s = n * 4 + i
            pu[s] = d[i] + pu[tbl[PREV_UP, s]]

    def take_down(n):
        d = []
        for i in range(4):
            s = n * 4 + i
            d.append(dot_nt(cols(dy_v, tbl[DN_COL, s]), gb[n, i]))
        for i in range(4):
            s = n * 4 + i
            pd[s] = d[i] + pd[tbl[PREV_DN, s]]

    def take(n, _):
        take_up(n)
        take_down(n)
        return 0

    for k, b in enumerate((0, 3, 1, 2)):
        for G in (A, B):
            for a in (3, 1):
                G.s1[a, b].wait_recv()
                G.s2[a, b].start()
        take(k, 0)
    for k, b in enumerate((0, 3, 1, 2)):
        lax.fori_loop(4 + 2 * k, 6 + 2 * k, take, 0)
    for k, b in enumerate((0, 3, 1, 2)):
        for G in (A, B):
            for a in (3, 1):
                G.s2[a, b].wait_recv()
        take(12 + k, 0)

    def part(dz, c, j):
        return pu[tbl[LAST_ROW, (((z + dz) % 8) * 2 + c) * 4 + j]]

    ZORDER = (4, 3, 5, 2, 6, 1, 7, 0)
    ex = {dz: message(xs.at[dz], rx.at[dz], mate) for dz in ZORDER}

    up_z = {}
    dn_z = {}
    for n in (4, 3, 2, 1):
        for h in range(2):
            hs = pl.ds(2 * h, 2)
            if n < 4 or h == 0:
                up_z[n, h] = message(zc.at[n, hs], rz.at[0, n - 1, hs], zp)
            if n < 4 or h == 1:
                dn_z[n, h] = message(zc.at[8 - n, hs], rz.at[1, n - 1, hs], zm)

    def ring(n):
        if n == 4:
            ex[4].wait_recv()
            for j in range(4):
                zc[4, j] = (part(4, core, j) + rx[4, j].astype(F32)).astype(BF16)
            up_z[4, 0].start()
            dn_z[4, 1].start()
            return
        ex[n].wait_recv()
        ex[8 - n].wait_recv()
        for k in range(2):
            for side, first in ((0, 1), (1, 0)):
                h = first if k == 0 else 1 - first
                came = (up_z, dn_z)[side]
                slot = n if side == 0 else 8 - n
                added = (n + 1, h) in came
                if added:
                    came[n + 1, h].wait_recv()
                for j in (2 * h, 2 * h + 1):
                    v = part(slot, core, j) + rx[slot, j].astype(F32)
                    if added:
                        v = v + rz[side, n, j].astype(F32)
                    zc[slot, j] = v.astype(BF16)
                came[n, h].start()

    def ring_end():
        ex[0].wait_recv()
        for h in range(2):
            up_z[1, h].wait_recv()
            dn_z[1, h].wait_recv()
            for j in (2 * h, 2 * h + 1):
                v = part(0, core, j) + rx[0, j].astype(F32)
                v = v + rz[0, 0, j].astype(F32) + rz[1, 0, j].astype(F32)
                gin_ref[:, j * TILE : (j + 1) * TILE] = v.astype(BF16)

    def grad_up(n):
        for i in range(4):
            s = n * 4 + i
            pa[n, i] = dot_nn(dpt_v[tbl[UP_COL, s]], cols(x_v, tbl[UP_ROW, s])).astype(BF16)

    def grad_down(n):
        for i in range(4):
            s = n * 4 + i
            pb[n, i] = dot_nn(ht_v[tbl[DN_ROW, s]], cols(dy_v, tbl[DN_COL, s])).astype(BF16)

    def add_half(p, n, h, r):
        for i in range(2):
            p[n, 2 * h + i] = (p[n, 2 * h + i].astype(F32) + r[i].astype(F32)).astype(BF16)

    class Scatter:
        def __init__(self, p, r1, r2, r3, r4, grad, first, second):
            (self.ap, self.am), (self.bp, self.bm) = first, second
            self.p, self.r1, self.r2, self.r3, self.r4, self.grad = p, r1, r2, r3, r4, grad
            at = lambda a, b: p.at[POS[a, b]]
            half = lambda a, b, h: p.at[POS[a, b], pl.ds(2 * h, 2)]
            self.m1 = {}
            self.m2 = {}
            for b in range(4):
                self.m1[1, b] = message(half(2, b, 0), r1.at[0, b], self.ap)
                self.m1[3, b] = message(half(2, b, 1), r1.at[1, b], self.am)
                self.m2[1, b] = message(at(1, b), r2.at[0, b], self.ap)
                self.m2[3, b] = message(at(3, b), r2.at[1, b], self.am)
            self.m3 = {
                1: message(half(0, 2, 0), r3.at[0], self.bp),
                3: message(half(0, 2, 1), r3.at[1], self.bm),
            }
            self.m4 = {
                1: message(at(0, 1), r4.at[0], self.bp),
                3: message(at(0, 3), r4.at[1], self.bm),
            }

        def far(self, b):
            self.grad(POS[2, b])
            self.m1[1, b].start()
            self.m1[3, b].start()

        def near(self, a, b):
            self.grad(POS[a, b])
            self.m1[a, b].wait_recv()
            h = 0 if a == 1 else 1
            add_half(self.p, POS[a, b], h, self.r1.at[h, b])
            self.m2[a, b].start()

        def total(self, b):
            self.m2[1, b].wait_recv()
            self.m2[3, b].wait_recv()
            n = POS[0, b]
            for i in range(4):
                v = self.p[n, i].astype(F32) + self.r2[0, b, i].astype(F32)
                v = v + self.r2[1, b, i].astype(F32)
                self.p[n, i] = v.astype(BF16)
            if b == 2:
                self.m3[1].start()
                self.m3[3].start()

        def turn(self, b):
            h = 0 if b == 1 else 1
            self.m3[b].wait_recv()
            add_half(self.p, POS[0, b], h, self.r3.at[h])
            self.m4[b].start()

        def end(self, out, flip):
            self.m4[1].wait_recv()
            self.m4[3].wait_recv()
            for i in range(4):
                v = self.p[POS[0, 0], i].astype(F32) + self.r4[0, i].astype(F32)
                v = v + self.r4[1, i].astype(F32)
                out[0, i] = (v.T if flip else v).astype(BF16)

    U = Scatter(pa, ra1, ra2, ra3, ra4, grad_up, (yp, ym), (xp, xm))
    D = Scatter(pb, rb1, rb2, rb3, rb4, grad_down, (xp, xm), (yp, ym))

    def activate(c, _):
        act, slope = gelu_parts(pu[tbl[LAST_UP, c]])
        slope_v[c] = slope
        ht_v[c] = act.T.astype(BF16)
        return 0

    def back(c, _):
        dpre = pd[tbl[LAST_DN, c]] * slope_v[c]
        dp_v[c] = dpre.astype(BF16)
        dpt_v[c] = dpre.T.astype(BF16)
        return 0

    lax.fori_loop(0, 16, activate, 0)
    for b in (2, 1, 3, 0):
        D.far(b)
    lax.fori_loop(0, 16, back, 0)
    for b in (2, 1, 3, 0):
        U.far(b)

    def take_in(n, _):
        d = []
        for i in range(4):
            s = n * 4 + i
            d.append(dot_nt(dp_v[tbl[UP_COL, s]], ga[n, i]))
        for i in range(4):
            s = n * 4 + i
            pu[s] = d[i] + pu[tbl[PREV_ROW, s]]
        return 0

    lax.fori_loop(0, 16, take_in, 0)

    for dz in ZORDER:
        for j in range(4):
            xs[dz, j] = part(dz, 1 - core, j).astype(BF16)
        ex[dz].start()

    ring(4)
    for b in (2, 1):
        for a in (1, 3):
            U.near(a, b)
            D.near(a, b)
    ring(3)
    for b in (3, 0):
        for a in (1, 3):
            U.near(a, b)
            D.near(a, b)
    ring(2)
    for b in (2, 1, 3, 0):
        grad_up(POS[0, b])
        grad_down(POS[0, b])
    for S in (U, D):
        S.total(2)
    ring(1)
    for b in (1, 3):
        for S in (U, D):
            S.total(b)
            S.turn(b)
    for S in (U, D):
        S.total(0)
    ring_end()
    U.end(gup_ref, True)
    D.end(gdn_ref, False)
    for copy in sent:
        copy.wait_send()
    assert count[0] <= 128


def hand_over(*refs):
    src, dst, held, sem = refs[0:3], refs[3:6], refs[6:9], refs[9]
    take = [pltpu.make_async_copy(src[i], held[i], sem.at[i]) for i in range(3)]
    give = [pltpu.make_async_copy(held[i], dst[i], sem.at[3 + i]) for i in range(3)]
    for copy in take:
        copy.start()
    for first, second in zip(take, give):
        first.wait()
        second.start()
    for copy in give:
        copy.wait()


def on_device(inputs, cotangent, up_tiles, up_rows, up_cols, down_tiles, down_rows, down_cols):
    tok = inputs.shape[0]
    width = inputs.shape[1]
    hbm = pl.BlockSpec(memory_space=pl.ANY)
    vmem = pl.BlockSpec(memory_space=pltpu.VMEM)
    smem = pl.BlockSpec(memory_space=pltpu.SMEM)
    tiles = lambda *n: pltpu.VMEM((*n, TILE, TILE), BF16)
    blocks = lambda *n: pltpu.VMEM((*n, tok, TILE), BF16)
    scatter_bufs = [tiles(2, 4, 2), tiles(2, 4, 4), tiles(2, 2), tiles(2, 4)]
    outs = (
        jax.ShapeDtypeStruct((tok, 4 * TILE), BF16),
        jax.ShapeDtypeStruct((1, 4, TILE, TILE), BF16),
        jax.ShapeDtypeStruct((1, 4, TILE, TILE), BF16),
    )
    results = pl.pallas_call(
        kernel,
        out_shape=outs,
        in_specs=[hbm, hbm, hbm, hbm, smem, smem, smem, smem],
        out_specs=(vmem, vmem, vmem),
        scratch_shapes=[
            blocks(width // TILE),
            blocks(width // TILE),
            tiles(16, 4),
            tiles(16, 4),
            pltpu.VMEM((4, 4, 8, TILE), jnp.int32),
            pltpu.VMEM((16, TILE), jnp.int32),
            pltpu.SMEM((16, TILE), jnp.int32),
            pltpu.VMEM((SLOTS + 1, tok, TILE), F32),
            pltpu.VMEM((SLOTS + 1, tok, TILE), F32),
            pltpu.VMEM((16, tok, TILE), F32),
            blocks(16),
            pltpu.VMEM((16, TILE, tok), BF16),
            pltpu.VMEM((16, TILE, tok), BF16),
            tiles(16, 4),
            tiles(16, 4),
            *scatter_bufs,
            *scatter_bufs,
            blocks(8, 4),
            blocks(8, 4),
            blocks(8, 4),
            blocks(2, 4, 4),
            pltpu.SemaphoreType.DMA((128,)),
            pltpu.SemaphoreType.DMA((128,)),
            pltpu.SemaphoreType.DMA((8,)),
        ],
        compiler_params=pltpu.CompilerParams(
            collective_id=0, has_side_effects=True, vmem_limit_bytes=60 * 1024 * 1024
        ),
    )(inputs, cotangent, up_tiles, down_tiles, up_rows, up_cols, down_rows, down_cols)
    return pl.pallas_call(
        hand_over,
        out_shape=outs,
        in_specs=[hbm] * 3,
        out_specs=(hbm,) * 3,
        scratch_shapes=[
            *(pltpu.VMEM(out.shape, out.dtype) for out in outs),
            pltpu.SemaphoreType.DMA((6,)),
        ],
        compiler_params=pltpu.CompilerParams(vmem_limit_bytes=63 * 1024 * 1024),
    )(*results)


def solution(mesh):
    placed = (
        P("fsdp", None),
        P("fsdp", None),
        P("tensor", "fsdp", None, None),
        P("tensor", "fsdp"),
        P("tensor", "fsdp"),
        P("tensor", "fsdp", None, None),
        P("tensor", "fsdp"),
        P("tensor", "fsdp"),
    )
    return jax.shard_map(
        on_device,
        mesh=mesh,
        in_specs=placed,
        out_specs=(
            P("fsdp", "tensor"),
            P("tensor", "fsdp", None, None),
            P("tensor", "fsdp", None, None),
        ),
        check_vma=False,
    )
```

```python
import jax
import jax.numpy as jnp
from jax import lax
from jax.experimental import pallas as pl
from jax.experimental.pallas import tpu as pltpu
from jax.sharding import PartitionSpec as P

TILE = 128
SLOTS = 64
MESH = pl.DeviceIdType.MESH
F32 = jnp.float32
BF16 = jnp.bfloat16

ORDER = (
    [(0, 0), (0, 3), (0, 1), (0, 2)]
    + [(a, b) for b in (0, 3, 1, 2) for a in (3, 1)]
    + [(2, b) for b in (0, 3, 1, 2)]
)
POS = {ab: n for n, ab in enumerate(ORDER)}
UP_ROW, UP_COL, DN_ROW, DN_COL, PREV_UP, PREV_DN, PREV_ROW, LAST_UP, LAST_DN, LAST_ROW = range(10)


def gelu_parts(pre):
    coef = 0.7978845608028654
    inner = coef * (pre + 0.044715 * pre * pre * pre)
    tanh_val = jnp.tanh(inner)
    act = 0.5 * pre * (1.0 + tanh_val)
    slope = 0.5 * (1.0 + tanh_val) + 0.5 * pre * (1.0 - tanh_val * tanh_val) * coef * (
        1.0 + 3.0 * 0.044715 * pre * pre
    )
    return act, slope


def dot_nn(a, b):
    return lax.dot_general(a, b, (((1,), (0,)), ((), ())), preferred_element_type=F32)


def dot_nt(a, b):
    return lax.dot_general(a, b, (((1,), (1,)), ((), ())), preferred_element_type=F32)


def kernel(
    x_hbm, dy_hbm, up_hbm, down_hbm, ur, uc, dr, dc,
    gin_ref, gup_ref, gdn_ref,
    x_v, dy_v, ga, gb, idx_v, tbl_v, tbl,
    pu, pd, slope_v, dp_v, dpt_v, ht_v,
    pa, pb, ra1, ra2, ra3, ra4, rb1, rb2, rb3, rb4,
    xs, rx, zc, rz,
    send_sem, recv_sem, loc_sem,
):
    f = lax.axis_index("fsdp")
    t = lax.axis_index("tensor")
    y, x = f // 4, f % 4
    z, core = t // 2, t % 2
    xp = {"fsdp": y * 4 + (x + 1) % 4}
    xm = {"fsdp": y * 4 + (x + 3) % 4}
    yp = {"fsdp": ((y + 1) % 4) * 4 + x}
    ym = {"fsdp": ((y + 3) % 4) * 4 + x}
    zp = {"tensor": ((z + 1) % 8) * 2 + core}
    zm = {"tensor": ((z + 7) % 8) * 2 + core}
    mate = {"tensor": z * 2 + 1 - core}

    count = [0]
    sent = []

    def message(src, dst, dev):
        n = count[0]
        count[0] += 1
        copy = pltpu.make_async_remote_copy(
            src_ref=src, dst_ref=dst, send_sem=send_sem.at[n], recv_sem=recv_sem.at[n],
            device_id=dev, device_id_type=MESH,
        )
        sent.append(copy)
        return copy

    own_a = pltpu.make_async_copy(up_hbm.at[0], ga.at[0], loc_sem.at[0])
    own_b = pltpu.make_async_copy(down_hbm.at[0], gb.at[0], loc_sem.at[1])
    get_x = pltpu.make_async_copy(x_v, x_v, loc_sem.at[2])
    get_dy = pltpu.make_async_copy(dy_v, dy_v, loc_sem.at[3])

    def fetch(c, _):
        src = pl.ds(pl.multiple_of(c * TILE, TILE), TILE)
        pltpu.make_async_copy(x_hbm.at[:, src], x_v.at[c], loc_sem.at[2]).start()
        pltpu.make_async_copy(dy_hbm.at[:, src], dy_v.at[c], loc_sem.at[3]).start()
        return 0

    own_a.start()
    own_b.start()

    barrier = pltpu.get_barrier_semaphore()
    for dev in (xp, xm, yp, ym, zp, zm, mate):
        pl.semaphore_signal(barrier, inc=1, device_id=dev, device_id_type=MESH)

    lane = lax.broadcasted_iota(jnp.int32, (8, TILE), 1)
    row = lax.broadcasted_iota(jnp.int32, (8, TILE), 0)
    own = jnp.zeros((8, TILE), jnp.int32)
    for r, ref in enumerate((ur, uc, dr, dc)):
        for i in range(4):
            own = jnp.where((row == r) & (lane == i), ref[0, i], own)
    idx_v[0, 0] = own
    own_a.wait()
    own_b.wait()
    pl.semaphore_wait(barrier, 7)

    class Gather:
        def __init__(self, g, first, second):
            (bp, bm), (ap, am) = first, second
            at = lambda a, b: g.at[POS[a, b]]
            half = lambda a, b, h: g.at[POS[a, b], pl.ds(2 * h, 2)]
            self.f1 = {3: message(at(0, 0), at(0, 3), bp), 1: message(at(0, 0), at(0, 1), bm)}
            self.f2 = {
                3: message(half(0, 3, 0), half(0, 2, 0), bp),
                1: message(half(0, 1, 1), half(0, 2, 1), bm),
            }
            self.s1 = {}
            self.s2 = {}
            for b in (0, 3, 1, 2):
                self.s1[3, b] = message(at(0, b), at(3, b), ap)
                self.s1[1, b] = message(at(0, b), at(1, b), am)
                self.s2[3, b] = message(half(3, b, 0), half(2, b, 0), ap)
                self.s2[1, b] = message(half(1, b, 1), half(2, b, 1), am)

    A = Gather(ga, (xp, xm), (yp, ym))
    B = Gather(gb, (yp, ym), (xp, xm))
    ix = {
        3: message(idx_v.at[0, 0], idx_v.at[0, 3], xp),
        1: message(idx_v.at[0, 0], idx_v.at[0, 1], xm),
        2: message(idx_v.at[0, 3], idx_v.at[0, 2], xp),
    }
    iy = {
        3: message(idx_v.at[0], idx_v.at[3], yp),
        1: message(idx_v.at[0], idx_v.at[1], ym),
        2: message(idx_v.at[3], idx_v.at[2], yp),
    }

    ix[3].start()
    ix[1].start()
    for b in (3, 1):
        A.f1[b].start()
        B.f1[b].start()
    for a in (3, 1):
        A.s1[a, 0].start()
        B.s1[a, 0].start()
    lax.fori_loop(0, 64, fetch, 0)
    ix[3].wait_recv()
    ix[2].start()
    zero = jnp.zeros((192, TILE), F32)
    pu[SLOTS] = zero
    pd[SLOTS] = zero
    ix[1].wait_recv()
    ix[2].wait_recv()
    iy[3].start()
    iy[1].start()

    for b in (3, 1):
        for G in (A, B):
            G.f1[b].wait_recv()
            G.f2[b].start()
            for a in (3, 1):
                G.s1[a, b].start()

    iy[3].wait_recv()
    iy[2].start()
    for G in (A, B):
        for b in (3, 1):
            G.f2[b].wait_recv()
        for a in (3, 1):
            G.s1[a, 2].start()
    iy[1].wait_recv()
    iy[2].wait_recv()

    both = jnp.zeros((8, TILE), jnp.int32)
    for v in range(4):
        for h in range(4):
            tile = idx_v[v, h]
            na, nb = POS[v, h], POS[h, v]
            moved_a = pltpu.roll(tile, 4 * na, 1) if na else tile
            moved_b = pltpu.roll(tile, 4 * nb, 1) if nb else tile
            both = both + jnp.where(row < 2, moved_a, jnp.where(row < 4, moved_b, 0))
    tbl_v[0:8] = both
    si = lax.broadcasted_iota(jnp.int32, (TILE, TILE), 0)
    li = lax.broadcasted_iota(jnp.int32, (TILE, TILE), 1)
    across = lambda r: jnp.broadcast_to(both[r : r + 1], (TILE, TILE))

    def chain(r):
        here = across(r)
        there = here.T
        prev = jnp.max(jnp.where((there == here) & (si < li), si, -1), axis=0, keepdims=True)
        last = jnp.max(jnp.where((there == li) & (si < SLOTS), si, -1), axis=0, keepdims=True)
        fix = lambda v: jnp.where(v < 0, SLOTS, v)
        return fix(prev), fix(last)

    prev_up, last_up = chain(UP_COL)
    prev_dn, last_dn = chain(DN_ROW)
    prev_row, last_row = chain(UP_ROW)
    tbl_v[PREV_UP : PREV_UP + 1] = prev_up
    tbl_v[PREV_DN : PREV_DN + 1] = prev_dn
    tbl_v[PREV_ROW : PREV_ROW + 1] = prev_row
    tbl_v[LAST_UP : LAST_UP + 1] = last_up
    tbl_v[LAST_DN : LAST_DN + 1] = last_dn
    tbl_v[LAST_ROW : LAST_ROW + 1] = last_row
    put = pltpu.make_async_copy(tbl_v, tbl, loc_sem.at[4])
    put.start()
    get_x.wait()
    get_dy.wait()
    put.wait()

    cols = lambda ref, n: ref[n]

    def take_up(n):
        d = []
        for i in range(4):
            s = n * 4 + i
            d.append(dot_nn(cols(x_v, tbl[UP_ROW, s]), ga[n, i]))
        for i in range(4):
            s = n * 4 + i
            pu[s] = d[i] + pu[tbl[PREV_UP, s]]

    def take_down(n):
        d = []
        for i in range(4):
            s = n * 4 + i
            d.append(dot_nt(cols(dy_v, tbl[DN_COL, s]), gb[n, i]))
        for i in range(4):
            s = n * 4 + i
            pd[s] = d[i] + pd[tbl[PREV_DN, s]]

    def take(n, _):
        take_up(n)
        take_down(n)
        return 0

    for k, b in enumerate((0, 3, 1, 2)):
        for G in (A, B):
            for a in (3, 1):
                G.s1[a, b].wait_recv()
                G.s2[a, b].start()
        take(k, 0)
    for k, b in enumerate((0, 3, 1, 2)):
        lax.fori_loop(4 + 2 * k, 6 + 2 * k, take, 0)
    for k, b in enumerate((0, 3, 1, 2)):
        for G in (A, B):
            for a in (3, 1):
                G.s2[a, b].wait_recv()
        take(12 + k, 0)

    def activate(c, _):
        act, slope = gelu_parts(pu[tbl[LAST_UP, c]])
        dpre = pd[tbl[LAST_DN, c]] * slope
        ht_v[c] = act.T.astype(BF16)
        dp_v[c] = dpre.astype(BF16)
        dpt_v[c] = dpre.T.astype(BF16)
        return 0

    lax.fori_loop(0, 16, activate, 0)

    def take_in(n, _):
        d = []
        for i in range(4):
            s = n * 4 + i
            d.append(dot_nt(dp_v[tbl[UP_COL, s]], ga[n, i]))
        for i in range(4):
            s = n * 4 + i
            pu[s] = d[i] + pu[tbl[PREV_ROW, s]]
        return 0

    lax.fori_loop(0, 16, take_in, 0)

    def part(dz, c, j):
        return pu[tbl[LAST_ROW, (((z + dz) % 8) * 2 + c) * 4 + j]]

    ZORDER = (4, 3, 5, 2, 6, 1, 7, 0)
    ex = {dz: message(xs.at[dz], rx.at[dz], mate) for dz in ZORDER}
    for dz in ZORDER:
        for j in range(4):
            xs[dz, j] = part(dz, 1 - core, j).astype(BF16)
        ex[dz].start()

    up_z = {}
    dn_z = {}
    for n in (4, 3, 2, 1):
        for h in range(2):
            hs = pl.ds(2 * h, 2)
            if n < 4 or h == 0:
                up_z[n, h] = message(zc.at[n, hs], rz.at[0, n - 1, hs], zp)
            if n < 4 or h == 1:
                dn_z[n, h] = message(zc.at[8 - n, hs], rz.at[1, n - 1, hs], zm)

    def ring(n):
        if n == 4:
            ex[4].wait_recv()
            for j in range(4):
                zc[4, j] = (part(4, core, j) + rx[4, j].astype(F32)).astype(BF16)
            up_z[4, 0].start()
            dn_z[4, 1].start()
            return
        ex[n].wait_recv()
        ex[8 - n].wait_recv()
        for k in range(2):
            for side, first in ((0, 1), (1, 0)):
                h = first if k == 0 else 1 - first
                came = (up_z, dn_z)[side]
                slot = n if side == 0 else 8 - n
                added = (n + 1, h) in came
                if added:
                    came[n + 1, h].wait_recv()
                for j in (2 * h, 2 * h + 1):
                    v = part(slot, core, j) + rx[slot, j].astype(F32)
                    if added:
                        v = v + rz[side, n, j].astype(F32)
                    zc[slot, j] = v.astype(BF16)
                came[n, h].start()

    def ring_end():
        ex[0].wait_recv()
        for h in range(2):
            up_z[1, h].wait_recv()
            dn_z[1, h].wait_recv()
            for j in (2 * h, 2 * h + 1):
                v = part(0, core, j) + rx[0, j].astype(F32)
                v = v + rz[0, 0, j].astype(F32) + rz[1, 0, j].astype(F32)
                gin_ref[:, j * TILE : (j + 1) * TILE] = v.astype(BF16)

    def grad_up(n):
        for i in range(4):
            s = n * 4 + i
            pa[n, i] = dot_nn(dpt_v[tbl[UP_COL, s]], cols(x_v, tbl[UP_ROW, s])).astype(BF16)

    def grad_down(n):
        for i in range(4):
            s = n * 4 + i
            pb[n, i] = dot_nn(ht_v[tbl[DN_ROW, s]], cols(dy_v, tbl[DN_COL, s])).astype(BF16)

    def add_half(p, n, h, r):
        for i in range(2):
            p[n, 2 * h + i] = (p[n, 2 * h + i].astype(F32) + r[i].astype(F32)).astype(BF16)

    class Scatter:
        def __init__(self, p, r1, r2, r3, r4, grad, first, second):
            (self.ap, self.am), (self.bp, self.bm) = first, second
            self.p, self.r1, self.r2, self.r3, self.r4, self.grad = p, r1, r2, r3, r4, grad
            at = lambda a, b: p.at[POS[a, b]]
            half = lambda a, b, h: p.at[POS[a, b], pl.ds(2 * h, 2)]
            self.m1 = {}
            self.m2 = {}
            for b in range(4):
                self.m1[1, b] = message(half(2, b, 0), r1.at[0, b], self.ap)
                self.m1[3, b] = message(half(2, b, 1), r1.at[1, b], self.am)
                self.m2[1, b] = message(at(1, b), r2.at[0, b], self.ap)
                self.m2[3, b] = message(at(3, b), r2.at[1, b], self.am)
            self.m3 = {
                1: message(half(0, 2, 0), r3.at[0], self.bp),
                3: message(half(0, 2, 1), r3.at[1], self.bm),
            }
            self.m4 = {
                1: message(at(0, 1), r4.at[0], self.bp),
                3: message(at(0, 3), r4.at[1], self.bm),
            }

        def far(self, b):
            self.grad(POS[2, b])
            self.m1[1, b].start()
            self.m1[3, b].start()

        def near(self, a, b):
            self.grad(POS[a, b])
            self.m1[a, b].wait_recv()
            h = 0 if a == 1 else 1
            add_half(self.p, POS[a, b], h, self.r1.at[h, b])
            self.m2[a, b].start()

        def total(self, b):
            self.m2[1, b].wait_recv()
            self.m2[3, b].wait_recv()
            n = POS[0, b]
            for i in range(4):
                v = self.p[n, i].astype(F32) + self.r2[0, b, i].astype(F32)
                v = v + self.r2[1, b, i].astype(F32)
                self.p[n, i] = v.astype(BF16)
            if b == 2:
                self.m3[1].start()
                self.m3[3].start()

        def turn(self, b):
            h = 0 if b == 1 else 1
            self.m3[b].wait_recv()
            add_half(self.p, POS[0, b], h, self.r3.at[h])
            self.m4[b].start()

        def end(self, out, flip):
            self.m4[1].wait_recv()
            self.m4[3].wait_recv()
            for i in range(4):
                v = self.p[POS[0, 0], i].astype(F32) + self.r4[0, i].astype(F32)
                v = v + self.r4[1, i].astype(F32)
                out[0, i] = (v.T if flip else v).astype(BF16)

    U = Scatter(pa, ra1, ra2, ra3, ra4, grad_up, (yp, ym), (xp, xm))
    D = Scatter(pb, rb1, rb2, rb3, rb4, grad_down, (xp, xm), (yp, ym))

    for b in (2, 1, 3, 0):
        U.far(b)
        D.far(b)
    ring(4)
    for b in (2, 1):
        for a in (1, 3):
            U.near(a, b)
            D.near(a, b)
    ring(3)
    for b in (3, 0):
        for a in (1, 3):
            U.near(a, b)
            D.near(a, b)
    ring(2)
    for b in (2, 1, 3, 0):
        grad_up(POS[0, b])
        grad_down(POS[0, b])
    for S in (U, D):
        S.total(2)
    ring(1)
    for b in (1, 3):
        for S in (U, D):
            S.total(b)
            S.turn(b)
    for S in (U, D):
        S.total(0)
    ring_end()
    U.end(gup_ref, True)
    D.end(gdn_ref, False)
    for copy in sent:
        copy.wait_send()
    assert count[0] <= 128


def hand_over(*refs):
    src, dst, held, sem = refs[0:3], refs[3:6], refs[6:9], refs[9]
    take = [pltpu.make_async_copy(src[i], held[i], sem.at[i]) for i in range(3)]
    give = [pltpu.make_async_copy(held[i], dst[i], sem.at[3 + i]) for i in range(3)]
    for copy in take:
        copy.start()
    for first, second in zip(take, give):
        first.wait()
        second.start()
    for copy in give:
        copy.wait()


def on_device(inputs, cotangent, up_tiles, up_rows, up_cols, down_tiles, down_rows, down_cols):
    tok = inputs.shape[0]
    width = inputs.shape[1]
    hbm = pl.BlockSpec(memory_space=pl.ANY)
    vmem = pl.BlockSpec(memory_space=pltpu.VMEM)
    smem = pl.BlockSpec(memory_space=pltpu.SMEM)
    tiles = lambda *n: pltpu.VMEM((*n, TILE, TILE), BF16)
    blocks = lambda *n: pltpu.VMEM((*n, tok, TILE), BF16)
    scatter_bufs = [tiles(2, 4, 2), tiles(2, 4, 4), tiles(2, 2), tiles(2, 4)]
    outs = (
        jax.ShapeDtypeStruct((tok, 4 * TILE), BF16),
        jax.ShapeDtypeStruct((1, 4, TILE, TILE), BF16),
        jax.ShapeDtypeStruct((1, 4, TILE, TILE), BF16),
    )
    results = pl.pallas_call(
        kernel,
        out_shape=outs,
        in_specs=[hbm, hbm, hbm, hbm, smem, smem, smem, smem],
        out_specs=(vmem, vmem, vmem),
        scratch_shapes=[
            blocks(width // TILE),
            blocks(width // TILE),
            tiles(16, 4),
            tiles(16, 4),
            pltpu.VMEM((4, 4, 8, TILE), jnp.int32),
            pltpu.VMEM((16, TILE), jnp.int32),
            pltpu.SMEM((16, TILE), jnp.int32),
            pltpu.VMEM((SLOTS + 1, tok, TILE), F32),
            pltpu.VMEM((SLOTS + 1, tok, TILE), F32),
            pltpu.VMEM((8, TILE), F32),
            blocks(16),
            pltpu.VMEM((16, TILE, tok), BF16),
            pltpu.VMEM((16, TILE, tok), BF16),
            tiles(16, 4),
            tiles(16, 4),
            *scatter_bufs,
            *scatter_bufs,
            blocks(8, 4),
            blocks(8, 4),
            blocks(8, 4),
            blocks(2, 4, 4),
            pltpu.SemaphoreType.DMA((128,)),
            pltpu.SemaphoreType.DMA((128,)),
            pltpu.SemaphoreType.DMA((8,)),
        ],
        compiler_params=pltpu.CompilerParams(
            collective_id=0, has_side_effects=True, vmem_limit_bytes=60 * 1024 * 1024
        ),
    )(inputs, cotangent, up_tiles, down_tiles, up_rows, up_cols, down_rows, down_cols)
    return pl.pallas_call(
        hand_over,
        out_shape=outs,
        in_specs=[hbm] * 3,
        out_specs=(hbm,) * 3,
        scratch_shapes=[
            *(pltpu.VMEM(out.shape, out.dtype) for out in outs),
            pltpu.SemaphoreType.DMA((6,)),
        ],
        compiler_params=pltpu.CompilerParams(vmem_limit_bytes=63 * 1024 * 1024),
    )(*results)


def solution(mesh):
    placed = (
        P("fsdp", None),
        P("fsdp", None),
        P("tensor", "fsdp", None, None),
        P("tensor", "fsdp"),
        P("tensor", "fsdp"),
        P("tensor", "fsdp", None, None),
        P("tensor", "fsdp"),
        P("tensor", "fsdp"),
    )
    return jax.shard_map(
        on_device,
        mesh=mesh,
        in_specs=placed,
        out_specs=(
            P("fsdp", "tensor"),
            P("tensor", "fsdp", None, None),
            P("tensor", "fsdp", None, None),
        ),
        check_vma=False,
    )
```
